32 devices in a mesh: segment: 4 (over y, x), seq: 8 (over z, core).
Axes of the slice: x: 2, y: 2, z: 4, core: 2. Of those that a mesh axis runs over, the one named last changes fastest.
Arguments:
- hidden: bfloat16 [4, 8192, 8192], P('segment', 'seq'), may hold values from -6 to 6
- span_lengths: int32 [4, 64], replicated, may hold values from 1 to 512, 8192 in all within a row
- section_of: int32 [4, 64], replicated, may hold values from 0 to 31
- section_live: int32 [32], P('seq'), may hold values 0 or 1
- w_in: bfloat16 [8192, 2048], P('seq'), may hold values from -0.5 to 0.5
- norm_gain: float32 [2048], replicated, may hold values from 0.5 to 1.5
- w_query: bfloat16 [2048, 2048], P(None, 'segment'), may hold values from -0.125 to 0.125
- w_key: bfloat16 [2048, 2048], P(None, 'segment'), may hold values from -0.125 to 0.125
- w_value: bfloat16 [2048, 2048], P(None, 'segment'), may hold values from -0.125 to 0.125
- w_out: bfloat16 [2048, 2048], P('segment'), may hold values from -0.125 to 0.125
Outputs:
- section_out: bfloat16 [32, 2048], P('seq')
The draws below stay inside these ranges and needn't reach their ends.
All inputs are finite; a program needn't handle non-finite values. No bound on the sum of `section_live` on one device may be relied on, other than what follows from the above.
Results may differ from the reference program's by a relative error of at most 0.007.
Values may be sent and summed in bfloat16 or wider, within the bound.
A program may use at most 128 MiB of HBM per device.

```python
import math
import jax
import jax.numpy as jnp
import numpy as np
from jax import lax

D = 8192
DS = 2048
HEADS = 16
HEAD_DIM = 128
SPAN_MAX = 512
DOCS = 4
L = 8192
NCH = 64
NSEC = 32


def with_ends(entries, own_key, smallest, largest):
    longest = entries.shape.index(max(entries.shape))
    spots = []
    for shift in (0, 1):
        where = [jax.random.randint(jax.random.fold_in(own_key, axis), (), 0, length) for axis, length in enumerate(entries.shape)]
        where[longest] = (where[longest] + shift) % entries.shape[longest]
        spots.append(tuple(where))
    return entries.at[spots[0]].set(smallest).at[spots[1]].set(largest)


def levels(rng, extent, pieces, low, top_value):
    gain = 1.0
    for position, blocks in pieces:
        steps = jax.random.uniform(jax.random.fold_in(jax.random.fold_in(rng, 6), position), (blocks,), jnp.float32, low / len(pieces), top_value / len(pieces))
        gain = gain * jnp.repeat(jnp.exp(steps), extent[position] // blocks).reshape((-1,) + (1,) * (len(extent) - 1 - position))
    return gain


def rank_table(amount, slope):
    weights = [(1 << 20) // math.isqrt(rank ** slope) + 1 for rank in range(1, amount + 1)]
    spread = 1 + sum(weights) // (1 << 30)
    return np.cumsum(np.array([max(1, weight // spread) for weight in weights]))


def skewed_ids(stream_key, shape, amount, skew):
    grid = rank_table(amount, skew)
    ticket = jax.random.randint(jax.random.fold_in(stream_key, 1), shape, 0, int(grid[amount - 1]))
    rank = jnp.searchsorted(jnp.asarray(grid, jnp.int32), ticket, side="right")
    return jax.random.permutation(jax.random.fold_in(stream_key, 2), amount)[rank].astype(jnp.int32)


def profile(count, total, most, slope):
    weights = [(1 << 20) // math.isqrt(standing ** slope) + 1 for standing in range(2, count + 1)]
    surplus, given = total - most - (count - 1), [1] * (count - 1)
    while surplus > 0:
        free = [i for i in range(count - 1) if given[i] < most]
        pool, remaining = sum([weights[i] for i in free]), surplus
        for i in free:
            extra = min(most - given[i], max(1, remaining * weights[i] // pool), surplus)
            given[i] = given[i] + extra
            surplus = surplus - extra
    return np.array([most] + given)


def ragged_sizes(rng, number_of, total, most, lean):
    if number_of == 2:
        one = jax.random.randint(rng, (), max(1, total - most), min(most, total - 1) + 1)
        return jnp.stack([one, total - one])
    lengths = jnp.asarray(profile(number_of, total, most, lean), jnp.int32)
    pairs = (number_of - 1) // 2
    donor, receiver = lengths[1:1 + 2 * pairs:2], lengths[2:2 + 2 * pairs:2]
    room = jnp.minimum(donor - 1, most - receiver)
    passed = jax.random.randint(jax.random.fold_in(rng, 1), (pairs,), 0, 1 << 20) % (room + 1)
    lengths = lengths.at[1:1 + 2 * pairs:2].set(donor - passed).at[2:2 + 2 * pairs:2].set(receiver + passed)
    return lengths[jax.random.permutation(jax.random.fold_in(rng, 2), number_of)]


def centred(rng, shape, deviation, most, shards=(), held_as=jnp.bfloat16):
    result = deviation * jax.random.normal(rng, shape, jnp.float32)
    if shards:
        result = result * levels(rng, shape, shards, -0.22, 0.18)
    return jnp.clip(result, -most, most).astype(held_as)


def setup_inputs(seed: int = 0) -> dict:
    keys = jax.random.split(jax.random.key(seed), 11)
    hidden = centred(keys[0], (DOCS, L, D), 1.0, 6.0, ((0, 4), (1, 8)))
    span_lengths = jax.vmap(lambda own: ragged_sizes(own, NCH, L, SPAN_MAX, 2))(jax.random.split(keys[1], DOCS)).reshape((DOCS, NCH)).astype(jnp.int32)
    section_of = with_ends(skewed_ids(keys[2], (DOCS, NCH), NSEC, 2), jax.random.fold_in(keys[2], 3), 0, NSEC - 1).astype(jnp.int32)
    section_live = with_ends((jax.random.randint(keys[3], (NSEC,), 0, 4) < 3).astype(jnp.int32), jax.random.fold_in(keys[3], 1), 0, 1)
    w_in = centred(keys[4], (D, DS), (D // 64) ** -0.5, 0.5, ((0, 8),))
    norm_gain = jnp.clip(1.0 + 0.1 * jax.random.normal(keys[5], (DS,), jnp.float32), 0.5, 1.5)
    w_query = centred(keys[6], (DS, DS), DS ** -0.5, 0.125, ((1, 4),))
    w_key = centred(keys[7], (DS, DS), DS ** -0.5, 0.125, ((1, 4),))
    w_value = centred(keys[8], (DS, DS), DS ** -0.5, 0.125, ((1, 4),))
    w_out = centred(keys[9], (DS, DS), DS ** -0.5, 0.125, ((0, 4),))
    return {"hidden": hidden, "span_lengths": span_lengths, "section_of": section_of, "section_live": section_live, "w_in": w_in, "norm_gain": norm_gain, "w_query": w_query, "w_key": w_key, "w_value": w_value, "w_out": w_out}


def reference(hidden, span_lengths, section_of, section_live, w_in, norm_gain, w_query, w_key, w_value, w_out):
    span_ends = jnp.cumsum(span_lengths, axis=1).astype(jnp.int32)
    span_starts = (span_ends - span_lengths).astype(jnp.int32)
    positions = jnp.arange(L, dtype=jnp.int32)

    def pool_document(packed):
        tokens, starts, stops = packed
        member = ((positions[None, :] >= starts[:, None]) & (positions[None, :] < stops[:, None])).astype(jnp.bfloat16)
        return jnp.dot(member, tokens, preferred_element_type=jnp.float32)
    span_sums = lax.map(pool_document, (hidden, span_starts, span_ends))
    span_means = span_sums / span_lengths[:, :, None].astype(jnp.float32)
    flat_sections = section_of.reshape(-1)
    onehot = (jnp.arange(NSEC, dtype=jnp.int32)[:, None] == flat_sections[None, :]).astype(jnp.float32)
    section_sums = jnp.dot(onehot, span_means.reshape(-1, D), precision=lax.Precision.HIGHEST)
    section_count = lax.optimization_barrier(jnp.sum(onehot, axis=1))
    section_pooled = (section_sums / jnp.maximum(section_count, 1.0)[:, None]).astype(jnp.bfloat16)
    section_in = jnp.dot(section_pooled, w_in, preferred_element_type=jnp.float32)
    scale = lax.rsqrt(lax.optimization_barrier(jnp.mean(section_in * section_in, axis=1, keepdims=True)) + 1e-05)
    normed = (section_in * scale * norm_gain[None, :]).astype(jnp.bfloat16)
    queries = jnp.dot(normed, w_query, preferred_element_type=jnp.float32).astype(jnp.bfloat16)
    keys_all = jnp.dot(normed, w_key, preferred_element_type=jnp.float32).astype(jnp.bfloat16)
    values_all = jnp.dot(normed, w_value, preferred_element_type=jnp.float32).astype(jnp.bfloat16)
    query_heads = queries.reshape(NSEC, HEADS, HEAD_DIM).astype(jnp.float32)
    key_heads = keys_all.reshape(NSEC, HEADS, HEAD_DIM).astype(jnp.float32)
    value_heads = values_all.reshape(NSEC, HEADS, HEAD_DIM).astype(jnp.float32)
    scores = jnp.einsum('qhd,khd->hqk', query_heads, key_heads) / jnp.sqrt(jnp.float32(HEAD_DIM))
    section_ids = jnp.arange(NSEC, dtype=jnp.int32)
    allowed = (section_live[None, :] > 0) | (section_ids[None, :] == section_ids[:, None])
    scores = jnp.where(allowed[None, :, :], scores, jnp.float32(-1e+30))
    probs = jax.nn.softmax(scores, axis=-1).astype(jnp.bfloat16)
    attended = jnp.einsum('hqk,khd->qhd', probs.astype(jnp.float32), value_heads).astype(jnp.bfloat16)
    attended = attended.reshape(NSEC, DS)
    mixed = section_in + jnp.dot(attended, w_out, preferred_element_type=jnp.float32)
    return mixed.astype(jnp.bfloat16)
```

```python
import functools
import jax
import jax.numpy as jnp
from jax import lax
from jax.experimental import pallas as pl
from jax.experimental.pallas import tpu as pltpu
from jax.sharding import PartitionSpec as P

HEAD_DIM = 128
MESH = pl.DeviceIdType.MESH
AHEAD = 4


def kernel(
    seg_n, seq_n,
    hidden, lengths_ref, sections_ref, live_ref, gain_ref, w_in, w_query, w_key, w_value, w_out,
    out_ref,
    hid, win, wqkv, wout, weights, pair_send, pair_recv, seg_own, seg_send, seg_recv,
    line_send, line_recv, pooled, proj_send, proj_recv, kv_send, kv_recv, kv_all,
    term_recv,
    load_sem, pair_ss, pair_rs, seg_ss, seg_rs, line_ss, line_rs, pool_ss, pool_rs,
    proj_ss, proj_rs, kv_ss, kv_rs, term_ss, term_rs,
):
    seg = lax.axis_index("segment")
    q = lax.axis_index("seq")
    core = lax.rem(q, 2)
    chip = lax.div(q, 2)
    chips = seq_n // 2
    partner = q + 1 - 2 * core
    tokens = hidden.shape[1]
    features = hid.shape[2]
    sub = features // seg_n
    here = live_ref.shape[0]
    sections = here * seq_n
    docs, spans = lengths_ref.shape
    f32, bf16 = jnp.float32, jnp.bfloat16

    def seg_peer(d):
        return lax.rem(seg + d, seg_n)

    def seq_peer(d):
        return lax.rem(q + d, seq_n)

    def dest_chip(k):
        return lax.rem(chip + 1 + k, chips)

    order = [("peer", 0)]
    for k in range(1, chips):
        order += [("peer", k), ("own", k - 1)]
    order.append(("own", chips - 1))

    def load(i):
        kind, k = order[i]
        block = dest_chip(k) * 2 + (core if kind == "own" else 1 - core)
        return pltpu.make_async_copy(
            hidden.at[0, :, pl.ds(pl.multiple_of(block * features, 128), features)],
            hid.at[i],
            load_sem.at[i],
        )

    n = len(order)
    weight_loads = [
        pltpu.make_async_copy(w_in, win, load_sem.at[n]),
        pltpu.make_async_copy(w_query, wqkv.at[0], load_sem.at[n + 1]),
        pltpu.make_async_copy(w_key, wqkv.at[1], load_sem.at[n + 2]),
        pltpu.make_async_copy(w_value, wqkv.at[2], load_sem.at[n + 3]),
        pltpu.make_async_copy(w_out, wout, load_sem.at[n + 4]),
    ]
    for i in range(min(AHEAD, n)):
        load(i).start()

    barrier = pltpu.get_barrier_semaphore()
    for d in range(1, seg_n):
        pl.semaphore_signal(barrier, inc=1, device_id=(seg_peer(d), q), device_id_type=MESH)
    for d in range(1, seq_n):
        pl.semaphore_signal(barrier, inc=1, device_id=(seg, seq_peer(d)), device_id_type=MESH)

    len_row = lengths_ref[pl.ds(seg, 1), :].astype(f32)
    sec_row = sections_ref[pl.ds(seg, 1), :]
    c_row = lax.broadcasted_iota(jnp.int32, (spans, spans), 0)
    c_col = lax.broadcasted_iota(jnp.int32, (spans, spans), 1)
    len_all = jnp.broadcast_to(len_row, (spans, spans))
    ends = jnp.sum(jnp.where(c_col <= c_row, len_all, 0.0), axis=1, keepdims=True)
    starts = jnp.sum(jnp.where(c_col < c_row, len_all, 0.0), axis=1, keepdims=True)
    position = (q * tokens + lax.broadcasted_iota(jnp.int32, (spans, tokens), 1)).astype(f32)
    member = jnp.where((position >= starts) & (position < ends), 1.0, 0.0).astype(bf16)
    inverse = 1.0 / len_row
    high = inverse.astype(bf16).astype(f32)
    low = inverse - high
    onehot = lax.broadcasted_iota(jnp.int32, (sections, spans), 0) == sec_row
    for t, part in enumerate((high, low)):
        spread = jnp.where(onehot, jnp.broadcast_to(part, (sections, spans)), 0.0).astype(bf16)
        weights[pl.ds(t * sections, sections), :] = jnp.dot(
            spread, member, preferred_element_type=f32
        ).astype(bf16)
    count = jnp.zeros((sections, 1), f32)
    for d in range(docs):
        same = lax.broadcasted_iota(jnp.int32, (sections, spans), 0) == sections_ref[d : d + 1, :]
        count += jnp.sum(jnp.where(same, 1.0, 0.0), axis=1, keepdims=True)
    count = jnp.maximum(count, 1.0)

    def pair_copy(k):
        return pltpu.make_async_remote_copy(
            pair_send.at[k], pair_recv.at[k], pair_ss.at[k], pair_rs.at[k],
            device_id=(seg, partner), device_id_type=MESH)

    def seg_copy(k, d):
        return pltpu.make_async_remote_copy(
            seg_send.at[k, seg_peer(d)], seg_recv.at[k, d - 1],
            seg_ss.at[k, d - 1], seg_rs.at[k, d - 1],
            device_id=(seg_peer(d), q), device_id_type=MESH)

    def line_copy(k):
        return pltpu.make_async_remote_copy(
            line_send.at[k], line_recv.at[k], line_ss.at[k], line_rs.at[k],
            device_id=(seg, dest_chip(k) * 2 + core), device_id_type=MESH)

    def seg_total(k):
        total = seg_own[k, seg]
        for d in range(1, seg_n):
            seg_copy(k, d).wait_recv()
            total += seg_recv[k, d - 1].astype(f32)
        return total

    for i, (kind, k) in enumerate(order):
        if i + AHEAD < n:
            load(i + AHEAD).start()
        elif i + AHEAD == n:
            for w in weight_loads:
                w.start()
        load(i).wait()
        both = jnp.dot(weights[...], hid[i], preferred_element_type=f32)
        part = both[:sections] + both[sections:]
        if i == 0:
            pl.semaphore_wait(barrier, seg_n + seq_n - 2)
        if kind == "peer":
            pair_send[k] = part
            pair_copy(k).start()
            continue
        pair_copy(k).wait_recv()
        part = part + pair_recv[k]
        for s in range(seg_n):
            piece = part[:, s * sub : (s + 1) * sub]
            seg_own[k, s] = piece
            seg_send[k, s] = piece.astype(bf16)
        for d in range(1, seg_n):
            seg_copy(k, d).start()
        if k > 0:
            line_send[k - 1] = seg_total(k - 1).astype(bf16)
            line_copy(k - 1).start()

    total = seg_total(chips - 1)
    for k in range(chips - 1):
        line_copy(k).wait_recv()
        total += line_recv[k].astype(f32)
    pooled[seg] = (total / count).astype(bf16)

    def pool_copy(d):
        return pltpu.make_async_remote_copy(
            pooled.at[seg], pooled.at[seg], pool_ss.at[d - 1], pool_rs.at[d - 1],
            device_id=(seg_peer(d), q), device_id_type=MESH)

    for d in range(1, seg_n):
        pool_copy(d).start()
    weight_loads[0].wait()
    for d in range(1, seg_n):
        pool_copy(d).wait_recv()
    projected = jnp.dot(pooled[0], win[0:sub, :], preferred_element_type=f32)
    for s in range(1, seg_n):
        projected += jnp.dot(
            pooled[s], win[s * sub : (s + 1) * sub, :], preferred_element_type=f32)
    for s in range(seq_n):
        proj_send[s] = projected[s * here : (s + 1) * here, :].astype(bf16)

    def proj_copy(d):
        return pltpu.make_async_remote_copy(
            proj_send.at[seq_peer(d)], proj_recv.at[q], proj_ss.at[d - 1], proj_rs.at[d - 1],
            device_id=(seg, seq_peer(d)), device_id_type=MESH)

    for d in range(1, seq_n):
        proj_copy(d).start()
    proj_recv[q] = proj_send[q]
    for w in weight_loads[1:]:
        w.wait()
    for d in range(1, seq_n):
        proj_copy(d).wait_recv()
    section_in = proj_recv[0].astype(f32)
    for s in range(1, seq_n):
        section_in += proj_recv[s].astype(f32)
    scale = lax.rsqrt(jnp.mean(section_in * section_in, axis=1, keepdims=True) + 1e-05)
    normed = (section_in * scale * gain_ref[...]).astype(bf16)
    columns = wqkv.shape[2]
    kv_send[:, 0:columns] = jnp.dot(normed, wqkv[1], preferred_element_type=f32).astype(bf16)
    kv_send[:, columns : 2 * columns] = jnp.dot(
        normed, wqkv[2], preferred_element_type=f32).astype(bf16)
    row = lax.broadcasted_iota(jnp.int32, (here, HEAD_DIM), 0)
    live = jnp.zeros((here, HEAD_DIM), f32)
    for i in range(here):
        live = jnp.where(row == i, live_ref[i].astype(f32), live)
    kv_send[:, 2 * columns :] = live.astype(bf16)

    def kv_copy(d):
        return pltpu.make_async_remote_copy(
            kv_send, kv_recv.at[q], kv_ss.at[d - 1], kv_rs.at[d - 1],
            device_id=(seg, seq_peer(d)), device_id_type=MESH)

    for d in range(1, seq_n):
        kv_copy(d).start()
    kv_recv[q] = kv_send[...]
    queries = jnp.dot(normed, wqkv[0], preferred_element_type=f32).astype(bf16)
    for d in range(1, seq_n):
        kv_copy(d).wait_recv()
    for s in range(seq_n):
        kv_all[s * here : (s + 1) * here, :] = kv_recv[s].astype(f32)
    across = (((1,), (1,)), ((), ()))
    live_all = kv_all[:, 2 * columns :].astype(bf16)
    live_sum = lax.dot_general(
        jnp.ones((here, HEAD_DIM), bf16), live_all, across, preferred_element_type=f32)
    own = q * here + lax.broadcasted_iota(jnp.int32, (here, sections), 0)
    allowed = (live_sum > 0) | (lax.broadcasted_iota(jnp.int32, (here, sections), 1) == own)
    terms = jnp.zeros((here, wout.shape[1]), f32)
    attended = []
    for h in range(columns // HEAD_DIM):
        lo = h * HEAD_DIM
        keys = kv_all[:, lo : lo + HEAD_DIM].astype(bf16)
        values = kv_all[:, columns + lo : columns + lo + HEAD_DIM].astype(bf16)
        scores = lax.dot_general(
            queries[:, lo : lo + HEAD_DIM], keys, across, preferred_element_type=f32)
        scores = jnp.where(allowed, scores / jnp.sqrt(f32(HEAD_DIM)), f32(-1e30))
        grown = jnp.exp(scores - jnp.max(scores, axis=1, keepdims=True))
        probs = (grown / jnp.sum(grown, axis=1, keepdims=True)).astype(bf16)
        attended.append(jnp.dot(probs, values, preferred_element_type=f32).astype(bf16))
    terms = jnp.dot(
        jnp.concatenate(attended, axis=1), wout[...], preferred_element_type=f32)
    term_recv[seg] = terms

    def term_copy(d):
        return pltpu.make_async_remote_copy(
            term_recv.at[seg], term_recv.at[seg], term_ss.at[d - 1], term_rs.at[d - 1],
            device_id=(seg_peer(d), q), device_id_type=MESH)

    for d in range(1, seg_n):
        term_copy(d).start()
    for d in range(1, seg_n):
        term_copy(d).wait_recv()
    combined = term_recv[0]
    for s in range(1, seg_n):
        combined += term_recv[s]
    out_ref[...] = (section_in + combined).astype(out_ref.dtype)

    for k in range(chips):
        pair_copy(k).wait_send()
        for d in range(1, seg_n):
            seg_copy(k, d).wait_send()
        if k < chips - 1:
            line_copy(k).wait_send()
    for d in range(1, seg_n):
        pool_copy(d).wait_send()
        term_copy(d).wait_send()
    for d in range(1, seq_n):
        proj_copy(d).wait_send()
        kv_copy(d).wait_send()


def shards(
    hidden, span_lengths, section_of, section_live, w_in, norm_gain, w_query, w_key, w_value, w_out
):
    seg_n, seq_n = lax.axis_size("segment"), lax.axis_size("seq")
    tokens, depth = hidden.shape[1:]
    here = section_live.shape[0]
    sections = here * seq_n
    chips = seq_n // 2
    features = depth // seq_n
    sub = features // seg_n
    width, columns = w_query.shape
    bf16, f32 = jnp.bfloat16, jnp.float32
    vmem = pl.BlockSpec(memory_space=pltpu.VMEM)
    smem = pl.BlockSpec(memory_space=pltpu.SMEM)
    hbm = pl.BlockSpec(memory_space=pl.ANY)
    dma = pltpu.SemaphoreType.DMA
    kv = 2 * columns + HEAD_DIM
    return pl.pallas_call(
        functools.partial(kernel, seg_n, seq_n),
        out_shape=jax.ShapeDtypeStruct((here, width), bf16),
        in_specs=[hbm, vmem, vmem, smem, vmem, hbm, hbm, hbm, hbm, hbm],
        out_specs=vmem,
        scratch_shapes=[
            pltpu.VMEM((seq_n, tokens, features), bf16),
            pltpu.VMEM(w_in.shape, bf16),
            pltpu.VMEM((3, width, columns), bf16),
            pltpu.VMEM(w_out.shape, bf16),
            pltpu.VMEM((2 * sections, tokens), bf16),
            pltpu.VMEM((chips, sections, features), f32),
            pltpu.VMEM((chips, sections, features), f32),
            pltpu.VMEM((chips, seg_n, sections, sub), f32),
            pltpu.VMEM((chips, seg_n, sections, sub), bf16),
            pltpu.VMEM((chips, seg_n - 1, sections, sub), bf16),
            pltpu.VMEM((chips - 1, sections, sub), bf16),
            pltpu.VMEM((chips - 1, sections, sub), bf16),
            pltpu.VMEM((seg_n, sections, sub), bf16),
            pltpu.VMEM((seq_n, here, width), bf16),
            pltpu.VMEM((seq_n, here, width), bf16),
            pltpu.VMEM((here, kv), bf16),
            pltpu.VMEM((seq_n, here, kv), bf16),
            pltpu.VMEM((sections, kv), f32),
            pltpu.VMEM((seg_n, here, width), f32),
            dma((seq_n + 5,)),
            dma((chips,)), dma((chips,)),
            dma((chips, seg_n - 1)), dma((chips, seg_n - 1)),
            dma((chips - 1,)), dma((chips - 1,)),
            dma((seg_n - 1,)), dma((seg_n - 1,)),
            dma((seq_n - 1,)), dma((seq_n - 1,)),
            dma((seq_n - 1,)), dma((seq_n - 1,)),
            dma((seg_n - 1,)), dma((seg_n - 1,)),
        ],
        compiler_params=pltpu.CompilerParams(
            collective_id=0, has_side_effects=True, vmem_limit_bytes=60 * 1024 * 1024
        ),
    )(
        hidden, span_lengths, section_of, section_live, norm_gain.reshape(1, -1),
        w_in, w_query, w_key, w_value, w_out,
    )


def solution(mesh):
    in_specs = (
        P("segment", "seq", None),
        P(),
        P(),
        P("seq"),
        P("seq", None),
        P(),
        P(None, "segment"),
        P(None, "segment"),
        P(None, "segment"),
        P("segment", None),
    )
    out_specs = P("seq", None)
    return jax.shard_map(shards, mesh=mesh, in_specs=in_specs, out_specs=out_specs, check_vma=False)
```

```python
import functools
import jax
import jax.numpy as jnp
from jax import lax
from jax.experimental import pallas as pl
from jax.experimental.pallas import tpu as pltpu
from jax.sharding import PartitionSpec as P

HEAD_DIM = 128
MESH = pl.DeviceIdType.MESH


def kernel(
    seg_n, seq_n,
    hidden, lengths_in, sections_in, live_in, gain_in, w_in, w_query, w_key, w_value, w_out,
    out_ref,
    lengths_ref, sections_ref, live_ref, gain_ref, hid, win, wqkv, wout, product, weights, pair_send, pair_recv, seg_own, seg_send, seg_recv,
    line_send, line_recv, pooled, proj_send, proj_recv, kv_send, kv_recv, kv_all,
    term_recv,
    load_sem, pair_ss, pair_rs, seg_ss, seg_rs, line_ss, line_rs, pool_ss, pool_rs,
    proj_ss, proj_rs, kv_ss, kv_rs, term_ss, term_rs,
):
    seg = lax.axis_index("segment")
    q = lax.axis_index("seq")
    core = lax.rem(q, 2)
    chip = lax.div(q, 2)
    chips = seq_n // 2
    partner = q + 1 - 2 * core
    tokens = hidden.shape[1]
    features = hid.shape[2]
    sub = features // seg_n
    here = live_ref.shape[0]
    sections = here * seq_n
    docs, spans = lengths_ref.shape
    f32, bf16 = jnp.float32, jnp.bfloat16

    def seg_peer(d):
        return lax.rem(seg + d, seg_n)

    def seq_peer(d):
        return lax.rem(q + d, seq_n)

    upper = lax.div(chip, max(chips // 2, 1))
    far_first = []
    for i in range(1, chips):
        k = upper * i + (1 - upper) * (chips - i)
        for c in range(2):
            far_first.append(lax.rem(lax.rem(chip + k, chips) * 2 + c - q + seq_n, seq_n))
    far_first.append(lax.rem(partner - q + seq_n, seq_n))

    def dest_chip(k):
        return lax.rem(chip + 1 + k, chips)

    barrier = pltpu.get_barrier_semaphore()
    for d in range(1, seg_n):
        pl.semaphore_signal(barrier, inc=1, device_id=(seg_peer(d), q), device_id_type=MESH)
    for d in range(1, seq_n):
        pl.semaphore_signal(barrier, inc=1, device_id=(seg, seq_peer(d)), device_id_type=MESH)

    order = [("peer", k) for k in range(chips)] + [("own", k) for k in range(chips)]

    def load(i):
        kind, k = order[i]
        block = dest_chip(k) * 2 + (core if kind == "own" else 1 - core)
        return pltpu.make_async_copy(
            hidden.at[0, :, pl.ds(pl.multiple_of(block * features, 128), features)],
            hid.at[i],
            load_sem.at[i],
        )

    n = len(order)
    weight_loads = [
        pltpu.make_async_copy(w_in, win, load_sem.at[n]),
        pltpu.make_async_copy(w_query, wqkv.at[0], load_sem.at[n + 1]),
        pltpu.make_async_copy(w_key, wqkv.at[1], load_sem.at[n + 2]),
        pltpu.make_async_copy(w_value, wqkv.at[2], load_sem.at[n + 3]),
        pltpu.make_async_copy(w_out, wout, load_sem.at[n + 4]),
    ]
    small_loads = [
        pltpu.make_async_copy(source, target, load_sem.at[n + 5 + i])
        for i, (source, target) in enumerate((
            (lengths_in, lengths_ref), (sections_in, sections_ref),
            (live_in, live_ref), (gain_in, gain_ref)))
    ]
    for c in small_loads:
        c.start()
    for i in range(chips):
        load(i).start()
    for c in small_loads:
        c.wait()

    len_row = lengths_ref[pl.ds(seg, 1), :].astype(f32)
    sec_row = sections_ref[pl.ds(seg, 1), :]
    c_row = lax.broadcasted_iota(jnp.int32, (spans, spans), 0)
    c_col = lax.broadcasted_iota(jnp.int32, (spans, spans), 1)
    len_all = jnp.broadcast_to(len_row, (spans, spans))
    ends = jnp.sum(jnp.where(c_col <= c_row, len_all, 0.0), axis=1, keepdims=True)
    starts = jnp.sum(jnp.where(c_col < c_row, len_all, 0.0), axis=1, keepdims=True)
    position = (q * tokens + lax.broadcasted_iota(jnp.int32, (spans, tokens), 1)).astype(f32)
    member = jnp.where((position >= starts) & (position < ends), 1.0, 0.0).astype(bf16)
    inverse = 1.0 / len_row
    high = inverse.astype(bf16).astype(f32)
    low = inverse - high
    onehot = lax.broadcasted_iota(jnp.int32, (sections, spans), 0) == sec_row
    for t, part in enumerate((high, low)):
        spread = jnp.where(onehot, jnp.broadcast_to(part, (sections, spans)), 0.0).astype(bf16)
        weights[pl.ds(t * sections, sections), :] = jnp.dot(
            spread, member, preferred_element_type=f32
        ).astype(bf16)
    count = jnp.zeros((sections, 1), f32)
    for d in range(docs):
        same = lax.broadcasted_iota(jnp.int32, (sections, spans), 0) == sections_ref[d : d + 1, :]
        count += jnp.sum(jnp.where(same, 1.0, 0.0), axis=1, keepdims=True)
    count = jnp.maximum(count, 1.0)

    def pair_copy(k):
        return pltpu.make_async_remote_copy(
            pair_send.at[k], pair_recv.at[k], pair_ss.at[k], pair_rs.at[k],
            device_id=(seg, partner), device_id_type=MESH)

    def seg_copy(k, d):
        return pltpu.make_async_remote_copy(
            seg_send.at[k, seg_peer(d)], seg_recv.at[k, d - 1],
            seg_ss.at[k, d - 1], seg_rs.at[k, d - 1],
            device_id=(seg_peer(d), q), device_id_type=MESH)

    def line_copy(k):
        return pltpu.make_async_remote_copy(
            line_send.at[k], line_recv.at[k], line_ss.at[k], line_rs.at[k],
            device_id=(seg, dest_chip(k) * 2 + core), device_id_type=MESH)

    def seg_total(k):
        total = seg_own[k, seg]
        for d in range(1, seg_n):
            seg_copy(k, d).wait_recv()
            total += seg_recv[k, d - 1].astype(f32)
        return total

    for i, (kind, k) in enumerate(order):
        if i < chips:
            load(i + chips).start()
        elif i == n - 2:
            for w in weight_loads:
                w.start()
        load(i).wait()
        both = jnp.dot(weights[...], hid[i], preferred_element_type=f32)
        part = both[:sections] + both[sections:]
        if kind == "peer":
            pair_send[k] = part
            if k == chips // 2:
                pl.semaphore_wait(barrier, seg_n + seq_n - 2)
                for j in range(k):
                    pair_copy(j).start()
            if k >= chips // 2:
                pair_copy(k).start()
            continue
        pair_copy(k).wait_recv()
        part = part + pair_recv[k]
        for s in range(seg_n):
            piece = part[:, s * sub : (s + 1) * sub]
            seg_own[k, s] = piece
            seg_send[k, s] = piece.astype(bf16)
        for d in range(1, seg_n):
            seg_copy(k, d).start()
        if k > 0:
            line_send[k - 1] = seg_total(k - 1).astype(bf16)
            line_copy(k - 1).start()

    total = seg_total(chips - 1)
    for k in range(chips - 1):
        line_copy(k).wait_recv()
        total += line_recv[k].astype(f32)
    pooled[seg] = (total / count).astype(bf16)

    def pool_copy(d):
        return pltpu.make_async_remote_copy(
            pooled.at[seg], pooled.at[seg], pool_ss.at[d - 1], pool_rs.at[d - 1],
            device_id=(seg_peer(d), q), device_id_type=MESH)

    for d in range(1, seg_n):
        pool_copy(d).start()
    weight_loads[0].wait()
    for d in range(seg_n):
        if d:
            pool_copy(d).wait_recv()
        slot = lax.rem(seg + seg_n - d, seg_n)
        product[slot] = jnp.dot(
            pooled[slot], win[pl.ds(pl.multiple_of(slot * sub, sub), sub), :],
            preferred_element_type=f32)
    projected = product[0]
    for s in range(1, seg_n):
        projected += product[s]
    for s in range(seq_n):
        proj_send[s] = projected[s * here : (s + 1) * here, :].astype(bf16)

    def proj_copy(d):
        return pltpu.make_async_remote_copy(
            proj_send.at[seq_peer(d)], proj_recv.at[q], proj_ss.at[d - 1], proj_rs.at[d - 1],
            device_id=(seg, seq_peer(d)), device_id_type=MESH)

    for d in far_first:
        proj_copy(d).start()
    proj_recv[q] = proj_send[q]
    for w in weight_loads[1:]:
        w.wait()
    for d in range(1, seq_n):
        proj_copy(d).wait_recv()
    section_in = proj_recv[0].astype(f32)
    for s in range(1, seq_n):
        section_in += proj_recv[s].astype(f32)
    scale = lax.rsqrt(jnp.mean(section_in * section_in, axis=1, keepdims=True) + 1e-05)
    normed = (section_in * scale * gain_ref[...]).astype(bf16)
    columns = wqkv.shape[2]
    kv_send[:, 0:columns] = jnp.dot(normed, wqkv[1], preferred_element_type=f32).astype(bf16)
    kv_send[:, columns : 2 * columns] = jnp.dot(
        normed, wqkv[2], preferred_element_type=f32).astype(bf16)
    row = lax.broadcasted_iota(jnp.int32, (here, HEAD_DIM), 0)
    live = jnp.zeros((here, HEAD_DIM), f32)
    for i in range(here):
        live = jnp.where(row == i, live_ref[i].astype(f32), live)
    kv_send[:, 2 * columns :] = live.astype(bf16)

    def kv_copy(d):
        return pltpu.make_async_remote_copy(
            kv_send, kv_recv.at[q], kv_ss.at[d - 1], kv_rs.at[d - 1],
            device_id=(seg, seq_peer(d)), device_id_type=MESH)

    for d in far_first:
        kv_copy(d).start()
    kv_recv[q] = kv_send[...]
    queries = jnp.dot(normed, wqkv[0], preferred_element_type=f32).astype(bf16)
    for d in range(1, seq_n):
        kv_copy(d).wait_recv()
    for s in range(seq_n):
        kv_all[s * here : (s + 1) * here, :] = kv_recv[s].astype(f32)
    across = (((1,), (1,)), ((), ()))
    live_all = kv_all[:, 2 * columns :].astype(bf16)
    live_sum = lax.dot_general(
        jnp.ones((here, HEAD_DIM), bf16), live_all, across, preferred_element_type=f32)
    own = q * here + lax.broadcasted_iota(jnp.int32, (here, sections), 0)
    allowed = (live_sum > 0) | (lax.broadcasted_iota(jnp.int32, (here, sections), 1) == own)
    terms = jnp.zeros((here, wout.shape[1]), f32)
    attended = []
    for h in range(columns // HEAD_DIM):
        lo = h * HEAD_DIM
        keys = kv_all[:, lo : lo + HEAD_DIM].astype(bf16)
        values = kv_all[:, columns + lo : columns + lo + HEAD_DIM].astype(bf16)
        scores = lax.dot_general(
            queries[:, lo : lo + HEAD_DIM], keys, across, preferred_element_type=f32)
        scores = jnp.where(allowed, scores / jnp.sqrt(f32(HEAD_DIM)), f32(-1e30))
        grown = jnp.exp(scores - jnp.max(scores, axis=1, keepdims=True))
        probs = (grown / jnp.sum(grown, axis=1, keepdims=True)).astype(bf16)
        attended.append(jnp.dot(probs, values, preferred_element_type=f32).astype(bf16))
    terms = jnp.dot(
        jnp.concatenate(attended, axis=1), wout[...], preferred_element_type=f32)
    term_recv[seg] = terms.astype(bf16)

    def term_copy(d):
        return pltpu.make_async_remote_copy(
            term_recv.at[seg], term_recv.at[seg], term_ss.at[d - 1], term_rs.at[d - 1],
            device_id=(seg_peer(d), q), device_id_type=MESH)

    for d in range(1, seg_n):
        term_copy(d).start()
    for d in range(1, seg_n):
        term_copy(d).wait_recv()
    combined = term_recv[0].astype(f32)
    for s in range(1, seg_n):
        combined += term_recv[s].astype(f32)
    out_ref[...] = (section_in + combined).astype(out_ref.dtype)

    for k in range(chips):
        pair_copy(k).wait_send()
        for d in range(1, seg_n):
            seg_copy(k, d).wait_send()
        if k < chips - 1:
            line_copy(k).wait_send()
    for d in range(1, seg_n):
        pool_copy(d).wait_send()
        term_copy(d).wait_send()
    for d in range(1, seq_n):
        proj_copy(d).wait_send()
        kv_copy(d).wait_send()


def shards(
    hidden, span_lengths, section_of, section_live, w_in, norm_gain, w_query, w_key, w_value, w_out
):
    seg_n, seq_n = lax.axis_size("segment"), lax.axis_size("seq")
    tokens, depth = hidden.shape[1:]
    here = section_live.shape[0]
    sections = here * seq_n
    chips = seq_n // 2
    features = depth // seq_n
    sub = features // seg_n
    width, columns = w_query.shape
    bf16, f32 = jnp.bfloat16, jnp.float32
    vmem = pl.BlockSpec(memory_space=pltpu.VMEM)
    hbm = pl.BlockSpec(memory_space=pl.ANY)
    dma = pltpu.SemaphoreType.DMA
    kv = 2 * columns + HEAD_DIM
    return pl.pallas_call(
        functools.partial(kernel, seg_n, seq_n),
        out_shape=jax.ShapeDtypeStruct((here, width), bf16),
        in_specs=[hbm] * 10,
        out_specs=vmem,
        scratch_shapes=[
            pltpu.VMEM(span_lengths.shape, jnp.int32),
            pltpu.VMEM(section_of.shape, jnp.int32),
            pltpu.SMEM((here,), jnp.int32),
            pltpu.VMEM((1, width), f32),
            pltpu.VMEM((seq_n, tokens, features), bf16),
            pltpu.VMEM(w_in.shape, bf16),
            pltpu.VMEM((3, width, columns), bf16),
            pltpu.VMEM(w_out.shape, bf16),
            pltpu.VMEM((seg_n, sections, width), f32),
            pltpu.VMEM((2 * sections, tokens), bf16),
            pltpu.VMEM((chips, sections, features), f32),
            pltpu.VMEM((chips, sections, features), f32),
            pltpu.VMEM((chips, seg_n, sections, sub), f32),
            pltpu.VMEM((chips, seg_n, sections, sub), bf16),
            pltpu.VMEM((chips, seg_n - 1, sections, sub), bf16),
            pltpu.VMEM((chips - 1, sections, sub), bf16),
            pltpu.VMEM((chips - 1, sections, sub), bf16),
            pltpu.VMEM((seg_n, sections, sub), bf16),
            pltpu.VMEM((seq_n, here, width), bf16),
            pltpu.VMEM((seq_n, here, width), bf16),
            pltpu.VMEM((here, kv), bf16),
            pltpu.VMEM((seq_n, here, kv), bf16),
            pltpu.VMEM((sections, kv), f32),
            pltpu.VMEM((seg_n, here, width), bf16),
            dma((seq_n + 9,)),
            dma((chips,)), dma((chips,)),
            dma((chips, seg_n - 1)), dma((chips, seg_n - 1)),
            dma((chips - 1,)), dma((chips - 1,)),
            dma((seg_n - 1,)), dma((seg_n - 1,)),
            dma((seq_n - 1,)), dma((seq_n - 1,)),
            dma((seq_n - 1,)), dma((seq_n - 1,)),
            dma((seg_n - 1,)), dma((seg_n - 1,)),
        ],
        compiler_params=pltpu.CompilerParams(
            collective_id=0, has_side_effects=True, vmem_limit_bytes=60 * 1024 * 1024
        ),
    )(
        hidden, span_lengths, section_of, section_live, norm_gain.reshape(1, -1),
        w_in, w_query, w_key, w_value, w_out,
    )


def solution(mesh):
    in_specs = (
        P("segment", "seq", None),
        P(),
        P(),
        P("seq"),
        P("seq", None),
        P(),
        P(None, "segment"),
        P(None, "segment"),
        P(None, "segment"),
        P("segment", None),
    )
    out_specs = P("seq", None)
    return jax.shard_map(shards, mesh=mesh, in_specs=in_specs, out_specs=out_specs, check_vma=False)
```
